32 devices in a mesh: section: 2 (over y), node: 4 (over z), lane: 4 (over x, core).
Axes of the slice: x: 2, y: 2, z: 4, core: 2. Of those that a mesh axis runs over, the one named last changes fastest.
Arguments:
- forward_input: bfloat16 [2, 1024, 2048], P('section', ('node', 'lane')), may hold values from -6 to 6
- forward_routes: int32 [2, 1024, 8], P('section', ('node', 'lane')), may hold values from 0 to 15, all different within a row; in each aligned block of 64 rows (0 to 63, 64 to 127, ..., all dimensions but the last counted through in order) at most 36 rows name the same one
- forward_gates: float32 [2, 1024, 8], P('section', ('node', 'lane')), may hold values from 0.05 to 0.4
- backward_input: bfloat16 [2, 1024, 2048], P('section', ('node', 'lane')), may hold values from -6 to 6
- backward_cotangent: bfloat16 [2, 1024, 2048], P('section', ('node', 'lane')), may hold values from -6 to 6
- backward_routes: int32 [2, 1024, 8], P('section', ('node', 'lane')), may hold values from 0 to 15, all different within a row; in each aligned block of 64 rows (0 to 63, 64 to 127, ..., all dimensions but the last counted through in order) at most 36 rows name the same one
- backward_gates: float32 [2, 1024, 8], P('section', ('node', 'lane')), may hold values from 0.05 to 0.4
- w_gate: bfloat16 [2, 16, 2048, 768], P('section', ('node', 'lane')), may hold values from -0.125 to 0.125
- w_up: bfloat16 [2, 16, 2048, 768], P('section', ('node', 'lane')), may hold values from -0.125 to 0.125
- w_down: bfloat16 [2, 16, 768, 2048], P('section', ('node', 'lane')), may hold values from -0.21875 to 0.21875
Outputs:
- next_input: bfloat16 [2, 1024, 2048], P('section', ('node', 'lane'))
- previous_gradient: bfloat16 [2, 1024, 2048], P('section', ('node', 'lane'))
The draws below stay inside these ranges and needn't reach their ends.
Inputs may be any that keep to these rules, and one draw needn't show every extreme that they name: `forward_routes`: each row names 8 different experts. Within the 64 rows of one device (aligned blocks), no expert is named by more than 36 rows, a bound that some block reaches. `backward_routes`: each row names 8 different experts. Within the 64 rows of one device (aligned blocks), no expert is named by more than 36 rows, a bound that some block reaches.
All inputs are finite; a program needn't handle non-finite values.
Results may differ from the reference program's by a relative error of at most 0.0064.
Values may be sent and summed in bfloat16 or wider, within the bound.
A program may use at most 128 MiB of HBM per device.

```python
import math
import jax
import jax.numpy as jnp
import numpy as np
from jax import lax

D = 2048
FF = 768
TOPK = 8
TOK_DEV = 64
EXPERTS = 16
TOKENS = 1024
CAP = 36
N_SECTION = 2
N_NODE = 4
N_LANE = 4


def shard_levels(rng, shape, cuts, smallest, top_value):
    gain = 1.0
    for position, blocks in cuts:
        steps = jax.random.uniform(jax.random.fold_in(jax.random.fold_in(rng, 6), position), (blocks,), jnp.float32, smallest / len(cuts), top_value / len(cuts))
        gain = gain * jnp.repeat(jnp.exp(steps), shape[position] // blocks).reshape((-1,) + (1,) * (len(shape) - 1 - position))
    return gain


def shared_out(key, own, number, rows, count, top, most, skew):
    ranking = jax.random.permutation(key, count)
    heavy_load, ordinary = portions_of(count, rows * top, most, skew, True), portions_of(count, rows * top, most, skew, False)
    places = jnp.arange(count)

    def named(sizes, turn):
        used = int((sizes > 0).sum())
        fixed = max(1, used // 4)
        passed = fixed + (places - fixed + turn * (used - fixed)) % max(1, count - fixed)
        return jnp.zeros((count,), jnp.int32).at[ranking[jnp.where(places < fixed, places, passed)]].set(jnp.asarray(sizes, jnp.int32))

    sizes = jnp.where(number % 4 == 0, named(heavy_load, number // 4), named(ordinary, number - number // 4 - 1))
    mixed = jax.random.permutation(jax.random.fold_in(own, 3), count)
    donor, sink = mixed[0:count // 2 * 2:2], mixed[1:count // 2 * 2:2]
    room = jnp.minimum(sizes[donor] - 1, most - sizes[sink]) // 2
    room = jnp.where((donor == ranking[0]) | (sink == ranking[0]) | (sizes[sink] == 0), 0, jnp.maximum(room, 0))
    passed = jax.random.randint(jax.random.fold_in(own, 4), (count // 2,), 0, 1 << 20) % (room + 1)
    sizes = sizes.at[donor].add(-passed).at[sink].add(passed)
    items = jnp.searchsorted(jnp.cumsum(sizes), jnp.arange(rows * top), side="right").astype(jnp.int32)
    grid = items.reshape(top, rows).T
    grid = grid[jax.random.permutation(jax.random.fold_in(own, 1), rows)]
    turn = jax.random.randint(jax.random.fold_in(own, 2), (rows, 1), 0, top)
    return jnp.take_along_axis(grid, (jnp.arange(top)[None, :] + turn) % top, axis=1)


def portions_of(number_of, total, bound, skew, full):
    weights = [(1 << 20) // math.isqrt(rank ** skew) + 1 for rank in range(1, number_of + 1)]
    largest = bound if full else min(bound, max(-(-total // number_of), total * weights[0] // sum(weights)))
    least = 1 if total - largest >= number_of - 1 else 0
    given, rest = [largest] + [least] * (number_of - 1), total - largest - least * (number_of - 1)
    while rest > 0:
        free = [i for i in range(1, number_of) if given[i] < largest] or [i for i in range(1, number_of) if given[i] < bound]
        mass, remaining = sum([weights[i] for i in free]), rest
        for i in free:
            extra = min(bound - given[i], max(1, remaining * weights[i] // mass), rest)
            given[i] = given[i] + extra
            rest = rest - extra
    return np.array(given)


def noise(rng, extent, spread, most, split=(), held_as=jnp.bfloat16):
    level = shard_levels(rng, extent, split, -0.22, 0.18) if split else 1.0
    entries = jax.random.normal(rng, extent, jnp.float32) * spread * level
    return jnp.minimum(jnp.maximum(entries, -most), most).astype(held_as)


def setup_inputs(seed: int = 0) -> dict:
    splits = jax.random.split(jax.random.key(seed), 11)
    forward_input = noise(splits[0], (N_SECTION, TOKENS, D), 1.0, 6.0, ((0, 2), (1, 16)))
    forward_routes_keys = jax.random.split(jax.random.fold_in(splits[1], 1), N_SECTION * TOKENS // TOK_DEV)
    forward_routes_turns = jax.random.permutation(jax.random.fold_in(splits[1], 3), N_SECTION * TOKENS // TOK_DEV)
    forward_routes = jax.vmap(lambda own, number: shared_out(jax.random.fold_in(splits[1], 2), own, number, TOK_DEV, EXPERTS, TOPK, CAP, 1))(forward_routes_keys, forward_routes_turns).reshape((N_SECTION, TOKENS, TOPK))
    forward_gates = jnp.clip(jnp.exp(math.log(0.4) - 2.0794415 * jax.random.uniform(splits[2], (N_SECTION, TOKENS, TOPK), jnp.float32) ** shard_levels(splits[2], (N_SECTION, TOKENS, TOPK), ((0, 2), (1, 16)), -0.2, 0.2)), 0.05, 0.4)
    backward_input = noise(splits[3], (N_SECTION, TOKENS, D), 1.0, 6.0, ((0, 2), (1, 16)))
    backward_cotangent = noise(splits[4], (N_SECTION, TOKENS, D), 1.0, 6.0, ((0, 2), (1, 16)))
    backward_routes_keys = jax.random.split(jax.random.fold_in(splits[5], 1), N_SECTION * TOKENS // TOK_DEV)
    backward_routes_turns = jax.random.permutation(jax.random.fold_in(splits[5], 3), N_SECTION * TOKENS // TOK_DEV)
    backward_routes = jax.vmap(lambda own, number: shared_out(jax.random.fold_in(splits[5], 2), own, number, TOK_DEV, EXPERTS, TOPK, CAP, 1))(backward_routes_keys, backward_routes_turns).reshape((N_SECTION, TOKENS, TOPK))
    backward_gates = jnp.clip(jnp.exp(math.log(0.4) - 2.0794415 * jax.random.uniform(splits[6], (N_SECTION, TOKENS, TOPK), jnp.float32) ** shard_levels(splits[6], (N_SECTION, TOKENS, TOPK), ((0, 2), (1, 16)), -0.2, 0.2)), 0.05, 0.4)
    w_gate = noise(splits[7], (N_SECTION, EXPERTS, D, FF), D ** -0.5, 0.125, ((0, 2), (1, 16)))
    w_up = noise(splits[8], (N_SECTION, EXPERTS, D, FF), D ** -0.5, 0.125, ((0, 2), (1, 16)))
    w_down = noise(splits[9], (N_SECTION, EXPERTS, FF, D), FF ** -0.5, 0.21875, ((0, 2), (1, 16)))
    return {"forward_input": forward_input, "forward_routes": forward_routes, "forward_gates": forward_gates, "backward_input": backward_input, "backward_cotangent": backward_cotangent, "backward_routes": backward_routes, "backward_gates": backward_gates, "w_gate": w_gate, "w_up": w_up, "w_down": w_down}


def expert_forward(rows, w_g, w_u, w_d):
    pre_gate = jnp.dot(rows, w_g, preferred_element_type=jnp.float32)
    pre_up = jnp.dot(rows, w_u, preferred_element_type=jnp.float32)
    hidden = (jax.nn.silu(pre_gate) * pre_up).astype(jnp.bfloat16)
    return jnp.dot(hidden, w_d, preferred_element_type=jnp.float32).astype(jnp.bfloat16)


def expert_backward(rows, grads, w_g, w_u, w_d):
    pre_gate = jnp.dot(rows, w_g, preferred_element_type=jnp.float32)
    pre_up = jnp.dot(rows, w_u, preferred_element_type=jnp.float32)
    grad_hidden = lax.dot_general(grads, w_d, (((1,), (1,)), ((), ())), preferred_element_type=jnp.float32)
    sigma = jax.nn.sigmoid(pre_gate)
    grad_gate = (grad_hidden * pre_up * sigma * (1.0 + pre_gate * (1.0 - sigma))).astype(jnp.bfloat16)
    grad_up = (grad_hidden * pre_gate * sigma).astype(jnp.bfloat16)
    total = lax.dot_general(grad_gate, w_g, (((1,), (1,)), ((), ())), preferred_element_type=jnp.float32)
    total = total + lax.dot_general(grad_up, w_u, (((1,), (1,)), ((), ())), preferred_element_type=jnp.float32)
    return total.astype(jnp.bfloat16)


def slot_index(routes):
    sources = N_NODE * N_LANE
    blocks = routes.reshape(sources, TOK_DEV * TOPK).astype(jnp.int32)
    onehot = (blocks[:, :, None] == jnp.arange(EXPERTS, dtype=jnp.int32)[None, None, :]).astype(jnp.int32)
    before = jnp.cumsum(onehot, axis=1) - onehot
    slot = jnp.sum(before * onehot, axis=2).astype(jnp.int32)
    anchor = jnp.arange(sources, dtype=jnp.int32)[:, None]
    return (blocks * (sources * CAP) + anchor * CAP + slot).reshape(-1).astype(jnp.int32)


def place(rows, index):
    buffer = jnp.zeros((EXPERTS * N_NODE * N_LANE * CAP, D), jnp.bfloat16)
    return buffer.at[index].set(rows).reshape(EXPERTS, N_NODE * N_LANE * CAP, D)


def forward_layer(tokens, routes, gates, w_g, w_u, w_d):
    index = slot_index(routes)
    buffer = place(jnp.repeat(tokens, TOPK, axis=0), index)
    outputs = lax.map(lambda item: expert_forward(*item), (buffer, w_g, w_u, w_d))
    picked = outputs.reshape(-1, D)[index].reshape(TOKENS, TOPK, D).astype(jnp.float32)
    return jnp.sum(picked * gates[:, :, None].astype(jnp.float32), axis=1).astype(jnp.bfloat16)


def backward_layer(tokens, cotangent, routes, gates, w_g, w_u, w_d):
    index = slot_index(routes)
    rows = place(jnp.repeat(tokens, TOPK, axis=0), index)
    scaled = (gates.reshape(-1)[:, None].astype(jnp.float32) * jnp.repeat(cotangent, TOPK, axis=0).astype(jnp.float32)).astype(jnp.bfloat16)
    grads = place(scaled, index)
    pieces = lax.map(lambda item: expert_backward(*item), (rows, grads, w_g, w_u, w_d))
    picked = pieces.reshape(-1, D)[index].reshape(TOKENS, TOPK, D).astype(jnp.float32)
    return jnp.sum(picked, axis=1).astype(jnp.bfloat16)


def reference(forward_input, forward_routes, forward_gates, backward_input, backward_cotangent, backward_routes, backward_gates, w_gate, w_up, w_down):
    outs_forward = []
    outs_backward = []
    for section in range(N_SECTION):
        outs_forward.append(forward_layer(forward_input[section], forward_routes[section], forward_gates[section], w_gate[section], w_up[section], w_down[section]))
        outs_backward.append(backward_layer(backward_input[section], backward_cotangent[section], backward_routes[section], backward_gates[section], w_gate[section], w_up[section], w_down[section]))
    layer_out = jnp.stack(outs_forward)
    input_grad = jnp.stack(outs_backward)
    return jnp.roll(layer_out, 1, axis=0), jnp.roll(input_grad, -1, axis=0)
```

```python
import jax
import jax.numpy as jnp
from jax import lax
from jax.sharding import PartitionSpec as P

GROUP = ("node", "lane")


def from_behind(value, axis, steps):
    count = lax.axis_size(axis)
    pairs = [(source, (source + steps) % count) for source in range(count)]
    return lax.ppermute(value, axis, pairs)


def coefficients(routes, gates, experts):
    hit = routes[:, :, None] == jnp.arange(experts, dtype=jnp.int32)[None, None, :]
    return jnp.sum(jnp.where(hit, gates[:, :, None], 0.0), axis=1)


def contract_last(a, b):
    return lax.dot_general(a, b, (((1,), (1,)), ((), ())), preferred_element_type=jnp.float32)


def local(
    forward_input,
    forward_routes,
    forward_gates,
    backward_input,
    backward_cotangent,
    backward_routes,
    backward_gates,
    w_gate,
    w_up,
    w_down,
):
    experts = lax.axis_size("node") * lax.axis_size("lane") * w_gate.shape[1]
    w_g, w_u, w_d = w_gate[0, 0], w_up[0, 0], w_down[0, 0]
    me = lax.axis_index(GROUP)

    coef = jnp.concatenate(
        [
            coefficients(forward_routes[0], forward_gates[0], experts),
            coefficients(backward_routes[0], backward_gates[0], experts),
        ],
        axis=1,
    )
    coef = lax.all_gather(coef, GROUP, axis=0, tiled=True)
    fwd_coef = lax.dynamic_slice_in_dim(coef, me, 1, axis=1)
    bwd_coef = lax.dynamic_slice_in_dim(coef, experts + me, 1, axis=1)

    fwd = lax.all_gather(forward_input[0], GROUP, axis=0, tiled=True)
    bwd = lax.all_gather(backward_input[0], GROUP, axis=0, tiled=True)
    cot = lax.all_gather(backward_cotangent[0], GROUP, axis=0, tiled=True)

    pre_gate = jnp.dot(fwd, w_g, preferred_element_type=jnp.float32)
    pre_up = jnp.dot(fwd, w_u, preferred_element_type=jnp.float32)
    hidden = (jax.nn.silu(pre_gate) * pre_up).astype(jnp.bfloat16)
    out = jnp.dot(hidden, w_d, preferred_element_type=jnp.float32)
    out = (out * fwd_coef).astype(jnp.bfloat16)
    layer_out = lax.psum_scatter(out, GROUP, scatter_dimension=0, tiled=True)

    pre_gate = jnp.dot(bwd, w_g, preferred_element_type=jnp.float32)
    pre_up = jnp.dot(bwd, w_u, preferred_element_type=jnp.float32)
    scaled = (bwd_coef * cot.astype(jnp.float32)).astype(jnp.bfloat16)
    grad_hidden = contract_last(scaled, w_d)
    sigma = jax.nn.sigmoid(pre_gate)
    grad_gate = (grad_hidden * pre_up * sigma * (1.0 + pre_gate * (1.0 - sigma))).astype(
        jnp.bfloat16
    )
    grad_up = (grad_hidden * pre_gate * sigma).astype(jnp.bfloat16)
    total = contract_last(grad_gate, w_g) + contract_last(grad_up, w_u)
    input_grad = lax.psum_scatter(
        total.astype(jnp.bfloat16), GROUP, scatter_dimension=0, tiled=True
    )
    next_input = from_behind(layer_out, "section", 1)
    previous_gradient = from_behind(input_grad, "section", -1)
    return (next_input[None], previous_gradient[None])


def solution(mesh):
    rows = P("section", GROUP, None)
    weights = P("section", GROUP, None, None)
    return jax.shard_map(
        local,
        mesh=mesh,
        in_specs=(rows,) * 7 + (weights,) * 3,
        out_specs=(rows, rows),
        check_vma=False,
    )
```

```python
import functools

import jax
import jax.numpy as jnp
from jax import lax
from jax.experimental import pallas as pl
from jax.experimental.pallas import tpu as pltpu
from jax.sharding import PartitionSpec as P

GROUP = ("node", "lane")
CORES = 2
MESH = pl.DeviceIdType.MESH


def position():
    node, lane = lax.axis_index("node"), lax.axis_index("lane")
    return node, lane // CORES, lane % CORES


def greet(peers):
    barrier = pltpu.get_barrier_semaphore()
    for cond, device in peers:
        @pl.when(cond)
        def _():
            pl.semaphore_signal(barrier, inc=1, device_id=device, device_id_type=MESH)
    pl.semaphore_wait(barrier, sum(jnp.where(cond, 1, 0) for cond, _ in peers))


def gather_kernel(n_node, n_x, count, *refs):
    ins, outs = refs[:count], refs[count : 2 * count]
    local_sem, recv, z_sem, x_sem, core_sem = refs[2 * count :]
    node, x, core = position()
    lane = x * CORES + core
    z_up, z_down = {"node": node + 1}, {"node": node - 1}
    x_up, x_down = {"lane": lane + CORES}, {"lane": lane - CORES}
    partner = {"lane": lane + 1 - 2 * core}
    has_up, has_down = node < n_node - 1, node > 0
    has_right, has_left = x < n_x - 1, x > 0
    greet(
        [
            (has_up, z_up),
            (has_down, z_down),
            (has_right, x_up),
            (has_left, x_down),
            (core < CORES, partner),
        ]
    )
    sends = []

    def send(cond, a, src, z, at_x, sem, device):
        where = outs[a].at[z, at_x * CORES + core]

        def copy():
            return pltpu.make_async_remote_copy(
                src_ref=where if src is None else src,
                dst_ref=where,
                send_sem=sem,
                recv_sem=recv.at[a, z, at_x * CORES + core],
                device_id=device,
                device_id_type=MESH,
            )

        @pl.when(cond)
        def _():
            copy().start()

        sends.append((cond, copy))

    def arrived(a, z, at_lane):
        where = outs[a].at[z, at_lane]
        pltpu.make_async_remote_copy(
            src_ref=where,
            dst_ref=where,
            send_sem=core_sem.at[a, 0, 0],
            recv_sem=recv.at[a, z, at_lane],
            device_id=partner,
            device_id_type=MESH,
        ).wait_recv()

    def along_x(cond, a, src, z):
        send(cond & has_right, a, src, z, x, x_sem.at[a, 0, z, x], x_up)
        send(cond & has_left, a, src, z, x, x_sem.at[a, 1, z, x], x_down)
        send(cond, a, src, z, x, core_sem.at[a, z, x], partner)

    always = core < CORES
    keeps = []
    for a in range(count):
        send(has_up, a, ins[a], node, x, z_sem.at[a, 0, node], z_up)
        send(has_down, a, ins[a], node, x, z_sem.at[a, 1, node], z_down)
        along_x(always, a, ins[a], node)
    for a in range(count):
        keep = pltpu.make_async_copy(ins[a], outs[a].at[node, lane], local_sem.at[a])
        keep.start()
        keeps.append(keep)
    for step in range(1, n_node):
        for a in range(count):
            below, above = node - step, node + step
            from_below, from_above = below >= 0, above < n_node

            @pl.when(from_below)
            def _():
                arrived(a, below, lane)

            send(from_below & has_up, a, None, below, x, z_sem.at[a, 0, below], z_up)
            along_x(from_below, a, None, below)

            @pl.when(from_above)
            def _():
                arrived(a, above, lane)

            send(from_above & has_down, a, None, above, x, z_sem.at[a, 1, above], z_down)
            along_x(from_above, a, None, above)
    for step in range(1, n_x):
        for a in range(count):
            for k in range(n_node):
                z = (node + k) % n_node
                for at_x, cond, go_on, way, device in (
                    (x - step, x - step >= 0, has_right, 0, x_up),
                    (x + step, x + step < n_x, has_left, 1, x_down),
                ):
                    @pl.when(cond)
                    def _():
                        arrived(a, z, at_x * CORES + core)

                    if n_x > 2:
                        send(cond & go_on, a, None, z, at_x, x_sem.at[a, way, z, at_x], device)
                    send(cond, a, None, z, at_x, core_sem.at[a, z, at_x], partner)
    for a in range(count):
        for k in range(n_node):
            for at_x in range(n_x):
                arrived(a, k, at_x * CORES + 1 - core)
    for cond, copy in sends:
        @pl.when(cond)
        def _():
            copy().wait_send()
    for keep in keeps:
        keep.wait()


def gather(*arrays):
    n_node, n_lane = lax.axis_size("node"), lax.axis_size("lane")
    n_x, count = n_lane // CORES, len(arrays)
    return pl.pallas_call(
        functools.partial(gather_kernel, n_node, n_x, count),
        out_shape=[jax.ShapeDtypeStruct((n_node, n_lane) + a.shape, a.dtype) for a in arrays],
        in_specs=[pl.BlockSpec(memory_space=pltpu.VMEM)] * count,
        out_specs=[pl.BlockSpec(memory_space=pl.ANY)] * count,
        scratch_shapes=[
            pltpu.SemaphoreType.DMA((count,)),
            pltpu.SemaphoreType.DMA((count, n_node, n_lane)),
            pltpu.SemaphoreType.DMA((count, 2, n_node)),
            pltpu.SemaphoreType.DMA((count, 2, n_node, n_x)),
            pltpu.SemaphoreType.DMA((count, n_node, n_x)),
        ],
        compiler_params=pltpu.CompilerParams(collective_id=0, has_side_effects=True),
    )(*arrays)


def scatter_kernel(n_section, n_node, n_x, count, *refs):
    parts, outs = refs[:count], refs[count : 2 * count]
    (own, core_in, x_in, z_in, final, local_sem, core_send, core_recv, x_send, x_recv, z_send,
     z_recv, y_send, y_recv) = refs[2 * count :]
    node, x, core = position()
    section = lax.axis_index("section")
    lane = x * CORES + core
    partner = {"lane": lane + 1 - 2 * core}
    z_up, z_down = {"node": node + 1}, {"node": node - 1}
    x_up, x_down = {"lane": lane + CORES}, {"lane": lane - CORES}
    after = {"section": (section + 1) % n_section}
    before = {"section": (section + n_section - 1) % n_section}
    has_up, has_down = node < n_node - 1, node > 0
    has_right, has_left = x < n_x - 1, x > 0
    always = core < CORES
    greet(
        [
            (has_up, z_up),
            (has_down, z_down),
            (has_right, x_up),
            (has_left, x_down),
            (always, partner),
            (always, after),
            (always, before),
        ]
    )

    def remote(src, dst, send_sem, recv_sem, device):
        return pltpu.make_async_remote_copy(
            src_ref=src,
            dst_ref=dst,
            send_sem=send_sem,
            recv_sem=recv_sem,
            device_id=device,
            device_id_type=MESH,
        )

    def add(target, *others):
        total = target[...].astype(jnp.float32)
        for other in others:
            total = total + other[...].astype(jnp.float32)
        target[...] = total.astype(target.dtype)

    sends = []

    def start(cond, make):
        @pl.when(cond)
        def _():
            make().start()

        sends.append((cond, make))

    owners = []
    for t in range(n_node - 1):
        owners.append((node + n_node - 1 - t, t >= node))
        owners.append((t + node - (n_node - 1), t + node >= n_node - 1))
    x_steps = [
        (t, x + n_x - 1 - t, t >= x, t + x - (n_x - 1), t + x >= n_x - 1) for t in range(n_x - 1)
    ]
    every = owners + [(node, always)]

    loads = []
    for a in range(count):
        load = pltpu.make_async_copy(parts[a].at[:, :, core], own.at[a], local_sem.at[a])
        load.start()
        loads.append(load)

    def core_copy(a, z, at_x):
        return remote(
            parts[a].at[z, at_x, 1 - core],
            core_in.at[a, z, at_x],
            core_send.at[a, z, at_x],
            core_recv.at[a, z, at_x],
            partner,
        )

    for a in range(count):
        for z, cond in every:
            for _, q_up, c_up, q_down, c_down in x_steps:
                start(cond & c_up, functools.partial(core_copy, a, z, q_up))
                start(cond & c_down, functools.partial(core_copy, a, z, q_down))
        for z, cond in every:
            start(cond, functools.partial(core_copy, a, z, x))

    def x_copy(a, z, q, slot, device):
        return remote(
            own.at[a, z, q], x_in.at[a, z, slot], x_send.at[a, z, q], x_recv.at[a, z, slot], device
        )

    def z_copy(a, z, slot, device):
        return remote(
            own.at[a, z, x], z_in.at[a, slot], z_send.at[a, z], z_recv.at[a, slot], device
        )

    for a in range(count):
        loads[a].wait()
        for z, cond in every:
            for t, q_up, c_up, q_down, c_down in x_steps:
                for q, c, more, slot, device in (
                    (q_up, c_up, has_left, q_up, x_up),
                    (q_down, c_down, has_right, None, x_down),
                ):
                    @pl.when(cond & c)
                    def _():
                        core_copy(a, z, q).wait_recv()
                        add(own.at[a, z, q], core_in.at[a, z, q])

                    if t > 0:
                        @pl.when(cond & c & more)
                        def _():
                            x_copy(a, z, q, q, partner).wait_recv()
                            add(own.at[a, z, q], x_in.at[a, z, q])

                    if slot is not None:
                        start(cond & c, functools.partial(x_copy, a, z, q, slot, device))
                    else:
                        near = q == x - 1
                        start(
                            cond & c & near, functools.partial(x_copy, a, z, q, n_x, device)
                        )
                        if n_x > 2:
                            start(
                                cond & c & (q < x - 1),
                                functools.partial(x_copy, a, z, q, q, device),
                            )

    def collect(a, z):
        core_copy(a, z, x).wait_recv()
        add(own.at[a, z, x], core_in.at[a, z, x])
        for c, slot in ((has_left, x), (has_right, n_x)):
            @pl.when(c)
            def _():
                x_copy(a, z, 0, slot, partner).wait_recv()
                add(own.at[a, z, x], x_in.at[a, z, slot])

    for a in range(count):
        for k, (z, cond) in enumerate(owners):
            going_up = k % 2 == 0

            @pl.when(cond)
            def _():
                collect(a, z)

            if k >= 2:
                @pl.when(cond & (has_down if going_up else has_up))
                def _():
                    z_copy(a, z, z, partner).wait_recv()
                    add(own.at[a, z, x], z_in.at[a, z])

            if going_up:
                start(cond, functools.partial(z_copy, a, z, z, z_up))
            else:
                start(cond & (z == node - 1), functools.partial(z_copy, a, z, n_node, z_down))
                if n_node > 2:
                    start(cond & (z < node - 1), functools.partial(z_copy, a, z, z, z_down))
        collect(a, node)

    def y_copy(a):
        return remote(
            final.at[a], outs[a], y_send.at[a], y_recv.at[a], after if a == 0 else before
        )

    for a in range(count):
        for c, slot in ((has_down, node), (has_up, n_node)):
            @pl.when(c)
            def _():
                z_copy(a, node, slot, partner).wait_recv()
                add(own.at[a, node, x], z_in.at[a, slot])
        final[a] = own[a, node, x]
        y_copy(a).start()
    for a in range(count):
        y_copy(a).wait()
    for cond, make in sends:
        @pl.when(cond)
        def _():
            make().wait_send()


def scatter(*parts):
    n_section, n_node = lax.axis_size("section"), lax.axis_size("node")
    n_x, count = lax.axis_size("lane") // CORES, len(parts)
    rows, width = parts[0].shape
    tok = rows // (n_node * n_x * CORES)
    dtype = parts[0].dtype
    block = (tok, width)
    dma = pltpu.SemaphoreType.DMA
    return pl.pallas_call(
        functools.partial(scatter_kernel, n_section, n_node, n_x, count),
        out_shape=[jax.ShapeDtypeStruct(block, dtype)] * count,
        in_specs=[pl.BlockSpec(memory_space=pl.ANY)] * count,
        out_specs=[pl.BlockSpec(memory_space=pltpu.VMEM)] * count,
        scratch_shapes=[
            pltpu.VMEM((count, n_node, n_x) + block, dtype),
            pltpu.VMEM((count, n_node, n_x) + block, dtype),
            pltpu.VMEM((count, n_node, n_x + 1) + block, dtype),
            pltpu.VMEM((count, n_node + 1) + block, dtype),
            pltpu.VMEM((count,) + block, dtype),
            dma((count,)),
            dma((count, n_node, n_x)),
            dma((count, n_node, n_x)),
            dma((count, n_node, n_x)),
            dma((count, n_node, n_x + 1)),
            dma((count, n_node)),
            dma((count, n_node + 1)),
            dma((count,)),
            dma((count,)),
        ],
        compiler_params=pltpu.CompilerParams(
            collective_id=1, has_side_effects=True, vmem_limit_bytes=67043328
        ),
    )(*(part.reshape((n_node, n_x, CORES) + block) for part in parts))


def coefficients(routes, gates, experts):
    hit = routes[:, :, None] == jnp.arange(experts, dtype=jnp.int32)[None, None, :]
    return jnp.sum(jnp.where(hit, gates[:, :, None], 0.0), axis=1)


def contract_last(a, b):
    return lax.dot_general(a, b, (((1,), (1,)), ((), ())), preferred_element_type=jnp.float32)


def local(
    forward_input,
    forward_routes,
    forward_gates,
    backward_input,
    backward_cotangent,
    backward_routes,
    backward_gates,
    w_gate,
    w_up,
    w_down,
):
    experts = lax.axis_size("node") * lax.axis_size("lane") * w_gate.shape[1]
    w_g, w_u, w_d = w_gate[0, 0], w_up[0, 0], w_down[0, 0]
    me = lax.axis_index(GROUP)

    coef = jnp.concatenate(
        [
            coefficients(forward_routes[0], forward_gates[0], experts),
            coefficients(backward_routes[0], backward_gates[0], experts),
        ],
        axis=1,
    )
    coef = jnp.pad(coef, ((0, 0), (0, -coef.shape[1] % 128)))
    tokens = forward_input.shape[1] * lax.axis_size("node") * lax.axis_size("lane")
    coef, fwd, bwd, cot = (
        array.reshape(tokens, -1)
        for array in gather(coef, forward_input[0], backward_input[0], backward_cotangent[0])
    )
    fwd_coef = lax.dynamic_slice_in_dim(coef, me, 1, axis=1)
    bwd_coef = lax.dynamic_slice_in_dim(coef, experts + me, 1, axis=1)

    pre_gate = jnp.dot(fwd, w_g, preferred_element_type=jnp.float32)
    pre_up = jnp.dot(fwd, w_u, preferred_element_type=jnp.float32)
    hidden = (jax.nn.silu(pre_gate) * pre_up).astype(jnp.bfloat16)
    out = jnp.dot(hidden, w_d, preferred_element_type=jnp.float32)
    out = (out * fwd_coef).astype(jnp.bfloat16)

    pre_gate = jnp.dot(bwd, w_g, preferred_element_type=jnp.float32)
    pre_up = jnp.dot(bwd, w_u, preferred_element_type=jnp.float32)
    scaled = (bwd_coef * cot.astype(jnp.float32)).astype(jnp.bfloat16)
    grad_hidden = contract_last(scaled, w_d)
    sigma = jax.nn.sigmoid(pre_gate)
    grad_gate = (grad_hidden * pre_up * sigma * (1.0 + pre_gate * (1.0 - sigma))).astype(
        jnp.bfloat16
    )
    grad_up = (grad_hidden * pre_gate * sigma).astype(jnp.bfloat16)
    total = contract_last(grad_gate, w_g) + contract_last(grad_up, w_u)
    next_input, previous_gradient = scatter(out, total.astype(jnp.bfloat16))
    return (next_input[None], previous_gradient[None])


def solution(mesh):
    rows = P("section", GROUP, None)
    weights = P("section", GROUP, None, None)
    return jax.shard_map(
        local,
        mesh=mesh,
        in_specs=(rows,) * 7 + (weights,) * 3,
        out_specs=(rows, rows),
        check_vma=False,
    )
```

```python
import functools

import jax
import jax.numpy as jnp
from jax import lax
from jax.experimental import pallas as pl
from jax.experimental.pallas import tpu as pltpu
from jax.sharding import PartitionSpec as P

GROUP = ("node", "lane")
CORES = 2
MESH = pl.DeviceIdType.MESH


def position():
    node, lane = lax.axis_index("node"), lax.axis_index("lane")
    return node, lane // CORES, lane % CORES


def greet(peers):
    barrier = pltpu.get_barrier_semaphore()
    for cond, device in peers:
        @pl.when(cond)
        def _():
            pl.semaphore_signal(barrier, inc=1, device_id=device, device_id_type=MESH)
    pl.semaphore_wait(barrier, sum(jnp.where(cond, 1, 0) for cond, _ in peers))


def gather_kernel(n_node, n_x, count, *refs):
    ins, outs = refs[:count], refs[count : 2 * count]
    local_sem, recv, z_sem, x_sem, core_sem = refs[2 * count :]
    node, x, core = position()
    lane = x * CORES + core
    z_up, z_down = {"node": node + 1}, {"node": node - 1}
    x_up, x_down = {"lane": lane + CORES}, {"lane": lane - CORES}
    partner = {"lane": lane + 1 - 2 * core}
    has_up, has_down = node < n_node - 1, node > 0
    has_right, has_left = x < n_x - 1, x > 0
    greet(
        [
            (has_up, z_up),
            (has_down, z_down),
            (has_right, x_up),
            (has_left, x_down),
            (core < CORES, partner),
        ]
    )
    sends = []

    def send(cond, a, src, z, at_x, sem, device):
        where = outs[a].at[z, at_x * CORES + core]

        def copy():
            return pltpu.make_async_remote_copy(
                src_ref=where if src is None else src,
                dst_ref=where,
                send_sem=sem,
                recv_sem=recv.at[a, z, at_x * CORES + core],
                device_id=device,
                device_id_type=MESH,
            )

        @pl.when(cond)
        def _():
            copy().start()

        sends.append((cond, copy))

    def arrived(a, z, at_lane):
        where = outs[a].at[z, at_lane]
        pltpu.make_async_remote_copy(
            src_ref=where,
            dst_ref=where,
            send_sem=core_sem.at[a, 0, 0],
            recv_sem=recv.at[a, z, at_lane],
            device_id=partner,
            device_id_type=MESH,
        ).wait_recv()

    def along_x(cond, a, src, z):
        send(cond & has_right, a, src, z, x, x_sem.at[a, 0, z, x], x_up)
        send(cond & has_left, a, src, z, x, x_sem.at[a, 1, z, x], x_down)
        send(cond, a, src, z, x, core_sem.at[a, z, x], partner)

    always = core < CORES
    keeps = []
    for a in range(count):
        send(has_up, a, ins[a], node, x, z_sem.at[a, 0, node], z_up)
        send(has_down, a, ins[a], node, x, z_sem.at[a, 1, node], z_down)
        along_x(always, a, ins[a], node)
    for a in range(count):
        keep = pltpu.make_async_copy(ins[a], outs[a].at[node, lane], local_sem.at[a])
        keep.start()
        keeps.append(keep)
    for step in range(1, n_node):
        for a in range(count):
            below, above = node - step, node + step
            from_below, from_above = below >= 0, above < n_node

            @pl.when(from_below)
            def _():
                arrived(a, below, lane)

            send(from_below & has_up, a, None, below, x, z_sem.at[a, 0, below], z_up)
            along_x(from_below, a, None, below)

            @pl.when(from_above)
            def _():
                arrived(a, above, lane)

            send(from_above & has_down, a, None, above, x, z_sem.at[a, 1, above], z_down)
            along_x(from_above, a, None, above)
    for step in range(1, n_x):
        for a in range(count):
            for k in range(n_node):
                z = (node + k) % n_node
                for at_x, cond, go_on, way, device in (
                    (x - step, x - step >= 0, has_right, 0, x_up),
                    (x + step, x + step < n_x, has_left, 1, x_down),
                ):
                    @pl.when(cond)
                    def _():
                        arrived(a, z, at_x * CORES + core)

                    if n_x > 2:
                        send(cond & go_on, a, None, z, at_x, x_sem.at[a, way, z, at_x], device)
                    send(cond, a, None, z, at_x, core_sem.at[a, z, at_x], partner)
    for a in range(count):
        for k in range(n_node):
            for at_x in range(n_x):
                arrived(a, k, at_x * CORES + 1 - core)
    for cond, copy in sends:
        @pl.when(cond)
        def _():
            copy().wait_send()
    for keep in keeps:
        keep.wait()


def gather(*arrays):
    n_node, n_lane = lax.axis_size("node"), lax.axis_size("lane")
    n_x, count = n_lane // CORES, len(arrays)
    return pl.pallas_call(
        functools.partial(gather_kernel, n_node, n_x, count),
        out_shape=[jax.ShapeDtypeStruct((n_node, n_lane) + a.shape, a.dtype) for a in arrays],
        in_specs=[pl.BlockSpec(memory_space=pltpu.VMEM)] * count,
        out_specs=[pl.BlockSpec(memory_space=pl.ANY)] * count,
        scratch_shapes=[
            pltpu.SemaphoreType.DMA((count,)),
            pltpu.SemaphoreType.DMA((count, n_node, n_lane)),
            pltpu.SemaphoreType.DMA((count, 2, n_node)),
            pltpu.SemaphoreType.DMA((count, 2, n_node, n_x)),
            pltpu.SemaphoreType.DMA((count, n_node, n_x)),
        ],
        compiler_params=pltpu.CompilerParams(collective_id=0, has_side_effects=True),
    )(*arrays)


def scatter_kernel(n_section, n_node, n_x, count, *refs):
    parts, outs = refs[:count], refs[count : 2 * count]
    (own, core_in, x_in, z_in, final, local_sem, core_send, core_recv, x_send, x_recv, z_send,
     z_recv, y_send, y_recv) = refs[2 * count :]
    node, x, core = position()
    section = lax.axis_index("section")
    lane = x * CORES + core
    partner = {"lane": lane + 1 - 2 * core}
    z_up, z_down = {"node": node + 1}, {"node": node - 1}
    x_up, x_down = {"lane": lane + CORES}, {"lane": lane - CORES}
    after = {"section": (section + 1) % n_section}
    before = {"section": (section + n_section - 1) % n_section}
    has_up, has_down = node < n_node - 1, node > 0
    has_right, has_left = x < n_x - 1, x > 0
    always = core < CORES
    greet(
        [
            (has_up, z_up),
            (has_down, z_down),
            (has_right, x_up),
            (has_left, x_down),
            (always, partner),
            (always, after),
            (always, before),
        ]
    )

    def remote(src, dst, send_sem, recv_sem, device):
        return pltpu.make_async_remote_copy(
            src_ref=src,
            dst_ref=dst,
            send_sem=send_sem,
            recv_sem=recv_sem,
            device_id=device,
            device_id_type=MESH,
        )

    def add(target, *others):
        total = target[...].astype(jnp.float32)
        for other in others:
            total = total + other[...].astype(jnp.float32)
        target[...] = total.astype(target.dtype)

    sends = []

    def start(cond, make):
        @pl.when(cond)
        def _():
            make().start()

        sends.append((cond, make))

    owners = []
    for t in range(n_node - 1):
        owners.append((node + n_node - 1 - t, t >= node))
        owners.append((t + node - (n_node - 1), t + node >= n_node - 1))
    x_steps = [
        (t, x + n_x - 1 - t, t >= x, t + x - (n_x - 1), t + x >= n_x - 1) for t in range(n_x - 1)
    ]
    every = owners + [(node, always)]

    loads = []
    for a in range(count):
        load = pltpu.make_async_copy(parts[a].at[:, :, core], own.at[a], local_sem.at[a])
        load.start()
        loads.append(load)

    def core_copy(a, z, at_x):
        return remote(
            parts[a].at[z, at_x, 1 - core],
            core_in.at[a, z, at_x],
            core_send.at[a, z, at_x],
            core_recv.at[a, z, at_x],
            partner,
        )

    for a in range(count):
        for z, cond in every:
            for _, q_up, c_up, q_down, c_down in x_steps:
                start(cond & c_up, functools.partial(core_copy, a, z, q_up))
                start(cond & c_down, functools.partial(core_copy, a, z, q_down))
        for z, cond in every:
            start(cond, functools.partial(core_copy, a, z, x))

    def x_copy(a, z, q, slot, device):
        return remote(
            own.at[a, z, q], x_in.at[a, z, slot], x_send.at[a, z, q], x_recv.at[a, z, slot], device
        )

    def z_copy(a, z, slot, device):
        return remote(
            own.at[a, z, x], z_in.at[a, slot], z_send.at[a, z], z_recv.at[a, slot], device
        )

    for a in range(count):
        loads[a].wait()
        for z, cond in every:
            for t, q_up, c_up, q_down, c_down in x_steps:
                for q, c, more, slot, device in (
                    (q_up, c_up, has_left, q_up, x_up),
                    (q_down, c_down, has_right, None, x_down),
                ):
                    @pl.when(cond & c)
                    def _():
                        core_copy(a, z, q).wait_recv()
                        add(own.at[a, z, q], core_in.at[a, z, q])

                    if t > 0:
                        @pl.when(cond & c & more)
                        def _():
                            x_copy(a, z, q, q, partner).wait_recv()
                            add(own.at[a, z, q], x_in.at[a, z, q])

                    if slot is not None:
                        start(cond & c, functools.partial(x_copy, a, z, q, slot, device))
                    else:
                        near = q == x - 1
                        start(
                            cond & c & near, functools.partial(x_copy, a, z, q, n_x, device)
                        )
                        if n_x > 2:
                            start(
                                cond & c & (q < x - 1),
                                functools.partial(x_copy, a, z, q, q, device),
                            )

    def collect(a, z):
        core_copy(a, z, x).wait_recv()
        add(own.at[a, z, x], core_in.at[a, z, x])
        for c, slot in ((has_left, x), (has_right, n_x)):
            @pl.when(c)
            def _():
                x_copy(a, z, 0, slot, partner).wait_recv()
                add(own.at[a, z, x], x_in.at[a, z, slot])

    for a in range(count):
        for k, (z, cond) in enumerate(owners):
            going_up = k % 2 == 0

            @pl.when(cond)
            def _():
                collect(a, z)

            if k >= 2:
                @pl.when(cond & (has_down if going_up else has_up))
                def _():
                    z_copy(a, z, z, partner).wait_recv()
                    add(own.at[a, z, x], z_in.at[a, z])

            if going_up:
                start(cond, functools.partial(z_copy, a, z, z, z_up))
            else:
                start(cond & (z == node - 1), functools.partial(z_copy, a, z, n_node, z_down))
                if n_node > 2:
                    start(cond & (z < node - 1), functools.partial(z_copy, a, z, z, z_down))
        collect(a, node)

    def y_copy(a):
        return remote(
            final.at[a], outs[a], y_send.at[a], y_recv.at[a], after if a == 0 else before
        )

    for a in range(count):
        for c, slot in ((has_down, node), (has_up, n_node)):
            @pl.when(c)
            def _():
                z_copy(a, node, slot, partner).wait_recv()
                add(own.at[a, node, x], z_in.at[a, slot])
        final[a] = own[a, node, x]
        y_copy(a).start()
    for a in range(count):
        y_copy(a).wait()
    for cond, make in sends:
        @pl.when(cond)
        def _():
            make().wait_send()


def scatter(*parts):
    n_section, n_node = lax.axis_size("section"), lax.axis_size("node")
    n_x, count = lax.axis_size("lane") // CORES, len(parts)
    rows, width = parts[0].shape
    tok = rows // (n_node * n_x * CORES)
    dtype = parts[0].dtype
    block = (tok, width)
    dma = pltpu.SemaphoreType.DMA
    return pl.pallas_call(
        functools.partial(scatter_kernel, n_section, n_node, n_x, count),
        out_shape=[jax.ShapeDtypeStruct(block, dtype)] * count,
        in_specs=[pl.BlockSpec(memory_space=pl.ANY)] * count,
        out_specs=[pl.BlockSpec(memory_space=pltpu.VMEM)] * count,
        scratch_shapes=[
            pltpu.VMEM((count, n_node, n_x) + block, dtype),
            pltpu.VMEM((count, n_node, n_x) + block, dtype),
            pltpu.VMEM((count, n_node, n_x + 1) + block, dtype),
            pltpu.VMEM((count, n_node + 1) + block, dtype),
            pltpu.VMEM((count,) + block, dtype),
            dma((count,)),
            dma((count, n_node, n_x)),
            dma((count, n_node, n_x)),
            dma((count, n_node, n_x)),
            dma((count, n_node, n_x + 1)),
            dma((count, n_node)),
            dma((count, n_node + 1)),
            dma((count,)),
            dma((count,)),
        ],
        compiler_params=pltpu.CompilerParams(
            collective_id=1, has_side_effects=True, vmem_limit_bytes=67043328
        ),
    )(*(part.reshape((n_node, n_x, CORES) + block) for part in parts))


def coefficients(routes, gates, experts):
    hit = routes[:, :, None] == jnp.arange(experts, dtype=jnp.int32)[None, None, :]
    return jnp.sum(jnp.where(hit, gates[:, :, None], 0.0), axis=1)


def contract_last(a, b):
    return lax.dot_general(a, b, (((1,), (1,)), ((), ())), preferred_element_type=jnp.float32)


def local(
    forward_input,
    forward_routes,
    forward_gates,
    backward_input,
    backward_cotangent,
    backward_routes,
    backward_gates,
    w_gate,
    w_up,
    w_down,
):
    experts = lax.axis_size("node") * lax.axis_size("lane") * w_gate.shape[1]
    w_g, w_u, w_d = w_gate[0, 0], w_up[0, 0], w_down[0, 0]
    me = lax.axis_index(GROUP)

    coef = jnp.concatenate(
        [
            coefficients(forward_routes[0], forward_gates[0], experts),
            coefficients(backward_routes[0], backward_gates[0], experts),
        ],
        axis=1,
    )
    coef = jnp.pad(coef, ((0, 0), (0, -coef.shape[1] % 128)))
    tokens = forward_input.shape[1] * lax.axis_size("node") * lax.axis_size("lane")
    coef, fwd, bwd, cot = (
        array.reshape(tokens, -1)
        for array in gather(coef, forward_input[0], backward_input[0], backward_cotangent[0])
    )
    fwd_coef = lax.dynamic_slice_in_dim(coef, me, 1, axis=1)
    bwd_coef = lax.dynamic_slice_in_dim(coef, experts + me, 1, axis=1)

    pre_gate = jnp.dot(fwd, w_g, preferred_element_type=jnp.float32)
    pre_up = jnp.dot(fwd, w_u, preferred_element_type=jnp.float32)
    hidden = (jax.nn.silu(pre_gate) * pre_up).astype(jnp.bfloat16)
    hidden = lax.optimization_barrier(hidden)
    out = jnp.dot(hidden, w_d, preferred_element_type=jnp.float32)
    out = (out * fwd_coef).astype(jnp.bfloat16)

    pre_gate = jnp.dot(bwd, w_g, preferred_element_type=jnp.float32)
    pre_up = jnp.dot(bwd, w_u, preferred_element_type=jnp.float32)
    grad_hidden = contract_last(cot, w_d) * bwd_coef
    sigma = jax.nn.sigmoid(pre_gate)
    grad_gate = (grad_hidden * pre_up * sigma * (1.0 + pre_gate * (1.0 - sigma))).astype(
        jnp.bfloat16
    )
    grad_up = (grad_hidden * pre_gate * sigma).astype(jnp.bfloat16)
    grad_gate, grad_up = lax.optimization_barrier((grad_gate, grad_up))
    total = contract_last(grad_gate, w_g) + contract_last(grad_up, w_u)
    next_input, previous_gradient = scatter(out, total.astype(jnp.bfloat16))
    return (next_input[None], previous_gradient[None])


def solution(mesh):
    rows = P("section", GROUP, None)
    weights = P("section", GROUP, None, None)
    return jax.shard_map(
        local,
        mesh=mesh,
        in_specs=(rows,) * 7 + (weights,) * 3,
        out_specs=(rows, rows),
        check_vma=False,
    )
```
